512 devices in a mesh: row: 32 (over z_hi, x, core), col: 16 (over y, z_lo).
Axes of the slice: x: 4, y: 4, z: 16 (z_hi: 4, z_lo: 4; z = z_hi * 4 + z_lo), core: 2. Of those that a mesh axis runs over, the one named last changes fastest.
Arguments:
- adjoint: bfloat16 [3, 128, 256, 512], P(None, 'col', 'row'), may hold values from -6 to 6
- velocity: bfloat16 [3, 128, 256, 512], P(None, 'col', 'row'), may hold values from -6 to 6
- control: bfloat16 [256, 512], P('row'), may hold values from -6 to 6
- deriv_x: bfloat16 [2, 512, 512], replicated, may hold values from -0.25 to 0.25
- deriv_y: bfloat16 [2, 256, 256], replicated, may hold values from -0.375 to 0.375
- deriv_z: bfloat16 [2, 128, 128], replicated, may hold values from -0.5 to 0.5
Outputs:
- adjoint_rate: bfloat16 [3, 128, 256, 512], P(None, 'col', 'row')
- control_grad: float32 [256, 512], P('row')
The draws below stay inside these ranges and needn't reach their ends.
All inputs are finite; a program needn't handle non-finite values.
Results may differ from the reference program's by a relative error of at most 0.009.
Values may be sent and summed in bfloat16 or wider, within the bound.
A program may use at most 64 MiB of HBM per device.

```python
import jax
import jax.numpy as jnp
from jax import lax

NX = 512
NY = 256
NZ = 128


def steps_of(stream_key, dims, split, least, largest):
    def one(axis_at, blocks):
        heights = jax.random.uniform(jax.random.fold_in(jax.random.fold_in(stream_key, 6), axis_at), (blocks,), jnp.float32, least / len(split), largest / len(split))
        return jnp.repeat(jnp.exp(heights), dims[axis_at] // blocks).reshape((-1,) + (1,) * (len(dims) - axis_at - 1))

    factor_of = one(*split[0])
    for cut in split[1:]:
        factor_of = factor_of * one(*cut)
    return factor_of


def scatter_about(key, extent, deviation, bound, pieces=(), kind=jnp.bfloat16):
    gain = steps_of(key, extent, pieces, -0.22, 0.18) if pieces else 1.0
    result = jax.random.normal(key, extent, jnp.float32) * deviation * gain
    return jnp.minimum(jnp.maximum(result, -bound), bound).astype(kind)


def setup_inputs(seed: int = 0) -> dict:
    key_list = jax.random.split(jax.random.key(seed), 7)
    adjoint = scatter_about(key_list[0], (3, NZ, NY, NX), 1.0, 6.0, ((1, 16), (2, 32)))
    velocity = scatter_about(key_list[1], (3, NZ, NY, NX), 1.0, 6.0, ((1, 16), (2, 32)))
    control = scatter_about(key_list[2], (NY, NX), 1.0, 6.0, ((0, 32),))
    deriv_x = scatter_about(key_list[3], (2, NX, NX), NX ** -0.5, 0.25)
    deriv_y = scatter_about(key_list[4], (2, NY, NY), NY ** -0.5, 0.375)
    deriv_z = scatter_about(key_list[5], (2, NZ, NZ), NZ ** -0.5, 0.5)
    return dict(adjoint=adjoint, velocity=velocity, control=control, deriv_x=deriv_x, deriv_y=deriv_y, deriv_z=deriv_z)


def directional(adjoint_in, velocity_in, matrices, component, grid_dim):
    letters = "abcd"
    source = letters[:grid_dim] + "p" + letters[grid_dim + 1:]
    target = "m" + letters[:grid_dim] + "q" + letters[grid_dim + 1:]
    stacked = jnp.einsum(source + ",mpq->" + target, adjoint_in.astype(jnp.float32), matrices.astype(jnp.float32))
    deriv_term = stacked[0]
    visc_term = stacked[1]
    speeds = velocity_in.astype(jnp.float32)
    summed = visc_term - speeds[component] * deriv_term
    summed = summed.at[component].add(-jnp.sum(speeds * deriv_term, axis=0))
    return summed.astype(jnp.bfloat16)


def reference(adjoint, velocity, control, deriv_x, deriv_y, deriv_z):
    def first_pass(block_index):
        start = block_index * 8
        piece_adj = lax.dynamic_slice_in_dim(adjoint, start, 8, 2)
        piece_vel = lax.dynamic_slice_in_dim(velocity, start, 8, 2)
        part_x = directional(piece_adj, piece_vel, deriv_x, 0, 3)
        part_z = directional(piece_adj, piece_vel, deriv_z, 2, 1)
        return jnp.stack([part_x, part_z])

    slabs = lax.map(first_pass, jnp.arange(NY // 8, dtype=jnp.int32))
    partials = jnp.moveaxis(slabs, 0, 3).reshape(2, 3, NZ, NY, NX)
    control_f = control.astype(jnp.float32)

    def second_pass(block_index):
        start = block_index * 8
        piece_adj = lax.dynamic_slice_in_dim(adjoint, start, 8, 1)
        piece_vel = lax.dynamic_slice_in_dim(velocity, start, 8, 1)
        earlier = lax.dynamic_slice_in_dim(partials, start, 8, 2)
        part_y = directional(piece_adj, piece_vel, deriv_y, 1, 2)
        side_sum = (part_y.astype(jnp.float32) + earlier[1].astype(jnp.float32)).astype(jnp.bfloat16)
        summed = earlier[0].astype(jnp.float32) + side_sum.astype(jnp.float32)
        forcing = control_f[None] * piece_adj[0].astype(jnp.float32)
        summed = summed.at[0].add(forcing)
        return summed.astype(jnp.bfloat16)

    planes = lax.map(second_pass, jnp.arange(NZ // 8, dtype=jnp.int32))
    adjoint_rate = jnp.moveaxis(planes, 0, 1).reshape(3, NZ, NY, NX)
    control_grad = jnp.sum(adjoint[0].astype(jnp.float32) * velocity[0].astype(jnp.float32), axis=0)
    return adjoint_rate, control_grad
```

```python
import functools

import jax
import jax.numpy as jnp
from jax import lax
from jax.experimental import pallas as pl
from jax.experimental.pallas import tpu as pltpu
from jax.sharding import PartitionSpec as P

BF = jnp.bfloat16
F32 = jnp.float32
ROWS = 32
COLS = 16
MESH = pl.DeviceIdType.MESH


def lanes(chunk):
    return pl.ds(pl.multiple_of(chunk * 128, 128), 128)


def remote(src, dst, send_sem, recv_sem, axis, peer):
    return pltpu.make_async_remote_copy(
        src_ref=src,
        dst_ref=dst,
        send_sem=send_sem,
        recv_sem=recv_sem,
        device_id={axis: peer},
        device_id_type=MESH,
    )


def wait_bytes(ref, sem):
    pltpu.make_async_copy(ref, ref, sem).wait()


def tendency(deriv, visc, speeds, d):
    mixed = speeds[0] * deriv[0] + speeds[1] * deriv[1] + speeds[2] * deriv[2]
    out = []
    for k in range(3):
        value = visc[k] - speeds[d] * deriv[k]
        if k == d:
            value = value - mixed
        out.append(value)
    return out


def kernel(
    adj, vel, ctl, dx, dy, dz, out, cg_out,
    adj_t, vel_t, row_adj, row_vel, col_adj, col_vel,
    py, pz, yback, zback, cg_mine, cg_all,
    base, gy, gz, dyt, dzt, send_sems, recv_sems,
):
    row = lax.axis_index("row")
    col = lax.axis_index("col")

    barrier = pltpu.get_barrier_semaphore()

    def greet(axis, me, n):
        def body(i, carry):
            peer = lax.rem(me + i, n)
            pl.semaphore_signal(barrier, inc=1, device_id={axis: peer}, device_id_type=MESH)
            return carry

        lax.fori_loop(1, n, body, 0)

    greet("row", row, ROWS)
    greet("col", col, COLS)

    for src, dst in ((adj, adj_t), (vel, vel_t)):
        for k in range(3):
            dst[:, k] = jnp.swapaxes(src[k].astype(F32), 0, 1).astype(BF)

    pl.semaphore_wait(barrier, ROWS - 1 + COLS - 1)

    def send_all(which, axis, me, n, view, slots):
        def body(i, carry):
            peer = lax.rem(me + i, n)
            remote(
                view(peer), slots.at[me], send_sems.at[which], recv_sems.at[which], axis, peer
            ).start()
            return carry

        lax.fori_loop(1, n, body, 0)
        pltpu.make_async_copy(view(me), slots.at[me], recv_sems.at[which]).start()

    def row_view(ref):
        return lambda r: ref.at[:, r // 4, :, lanes(lax.rem(r, 4))]

    def col_view(ref):
        return lambda c: ref.at[pl.ds(c // 4 * 2, 2), :, :, lanes(lax.rem(c, 4))]

    send_all(0, "row", row, ROWS, row_view(adj), row_adj)
    send_all(1, "row", row, ROWS, row_view(vel), row_vel)
    send_all(2, "col", col, COLS, col_view(adj_t), col_adj)
    send_all(3, "col", col, COLS, col_view(vel_t), col_vel)

    for m in range(2):
        dyt[m * 256 : m * 256 + 256, :] = dy[m].astype(F32).T.astype(BF)
        dzt[m * 128 : m * 128 + 128, :] = dz[m].astype(F32).T.astype(BF)

    flat = adj[...].astype(F32).reshape(192, 512).astype(BF)
    for c in range(2):
        cols = slice(c * 256, c * 256 + 256)
        g0 = jnp.dot(flat, dx[0, :, cols], preferred_element_type=F32)
        g1 = jnp.dot(flat, dx[1, :, cols], preferred_element_type=F32)
        speeds = [vel[k, :, :, cols].astype(F32).reshape(64, 256) for k in range(3)]
        parts = tendency(
            [g0[k * 64 : k * 64 + 64] for k in range(3)],
            [g1[k * 64 : k * 64 + 64] for k in range(3)],
            speeds,
            0,
        )
        for k in range(3):
            value = parts[k].astype(BF).astype(F32).reshape(8, 8, 256)
            if k == 0:
                value = value + ctl[:, cols].astype(F32)[None] * adj[0, :, :, cols].astype(F32)
            base[k, :, :, cols] = value

    wait_bytes(row_adj, recv_sems.at[0])
    lines = jnp.concatenate(
        [row_adj[:, k].astype(F32).reshape(256, 128) for k in range(3)], axis=1
    ).astype(BF)
    gy[...] = jnp.dot(dyt[...], lines, preferred_element_type=F32)
    wait_bytes(row_vel, recv_sems.at[1])
    for c in range(8):
        at = slice(c * 4, c * 4 + 4)
        rows0 = slice(c * 32, c * 32 + 32)
        rows1 = slice(256 + c * 32, 256 + c * 32 + 32)
        parts = tendency(
            [gy[rows0, k * 128 : k * 128 + 128] for k in range(3)],
            [gy[rows1, k * 128 : k * 128 + 128] for k in range(3)],
            [row_vel[at, k].astype(F32).reshape(32, 128) for k in range(3)],
            1,
        )
        for k in range(3):
            py[at, k] = parts[k].reshape(4, 8, 128).astype(BF)
    send_all(4, "row", row, ROWS, lambda r: py.at[r], yback)

    wait_bytes(col_adj, recv_sems.at[2])
    lines = jnp.concatenate(
        [col_adj[:, y, k].astype(F32).reshape(128, 128) for y in range(2) for k in range(3)],
        axis=1,
    ).astype(BF)
    gz[...] = jnp.dot(dzt[...], lines, preferred_element_type=F32)
    wait_bytes(col_vel, recv_sems.at[3])
    for y in range(2):
        cg_mine[y : y + 1, :] = jnp.sum(
            (col_adj[:, y, 0].astype(F32) * col_vel[:, y, 0].astype(F32)).reshape(128, 128),
            axis=0,
            keepdims=True,
        )
    for c in range(4):
        at = slice(c * 4, c * 4 + 4)
        rows0 = slice(c * 32, c * 32 + 32)
        rows1 = slice(128 + c * 32, 128 + c * 32 + 32)
        for y in range(2):
            first = y * 3
            parts = tendency(
                [gz[rows0, (first + k) * 128 : (first + k + 1) * 128] for k in range(3)],
                [gz[rows1, (first + k) * 128 : (first + k + 1) * 128] for k in range(3)],
                [col_vel[at, y, k].astype(F32).reshape(32, 128) for k in range(3)],
                2,
            )
            for k in range(3):
                pz[at, y, k] = parts[k].reshape(4, 8, 128).astype(BF)
    send_all(5, "col", col, COLS, lambda c: pz.at[c], zback)
    send_all(6, "col", col, COLS, lambda c: cg_mine, cg_all)

    wait_bytes(yback, recv_sems.at[4])
    wait_bytes(zback, recv_sems.at[5])
    for x in range(4):
        cols = slice(x * 128, x * 128 + 128)
        for k in range(3):
            span = jnp.stack(
                [zback[(y // 2) * 4 + x, y % 2, k].astype(F32) for y in range(8)], axis=0
            )
            span = jnp.swapaxes(span, 0, 1)
            normal = jnp.stack([yback[z * 4 + x, k].astype(F32) for z in range(8)], axis=0)
            side = (normal + span).astype(BF).astype(F32)
            out[k, :, :, cols] = (base[k, :, :, cols] + side).astype(BF)
    wait_bytes(cg_all, recv_sems.at[6])
    for c in range(COLS):
        yp, x = c // 4, c % 4
        cg_out[yp * 2 : yp * 2 + 2, x * 128 : x * 128 + 128] = cg_all[c]

    for which, slots in enumerate((row_adj, row_vel, col_adj, col_vel, yback, zback, cg_all)):
        wait_bytes(slots.at[pl.ds(0, slots.shape[0] - 1)], send_sems.at[which])


def on_device(adjoint, velocity, control, deriv_x, deriv_y, deriv_z):
    vmem = pl.BlockSpec(memory_space=pltpu.VMEM)
    return pl.pallas_call(
        kernel,
        out_shape=(
            jax.ShapeDtypeStruct((3, 8, 8, 512), BF),
            jax.ShapeDtypeStruct((8, 512), F32),
        ),
        in_specs=[vmem] * 6,
        out_specs=(vmem, vmem),
        scratch_shapes=[
            pltpu.VMEM((8, 3, 8, 512), BF),
            pltpu.VMEM((8, 3, 8, 512), BF),
            pltpu.VMEM((ROWS, 3, 8, 128), BF),
            pltpu.VMEM((ROWS, 3, 8, 128), BF),
            pltpu.VMEM((COLS, 2, 3, 8, 128), BF),
            pltpu.VMEM((COLS, 2, 3, 8, 128), BF),
            pltpu.VMEM((ROWS, 3, 8, 128), BF),
            pltpu.VMEM((COLS, 2, 3, 8, 128), BF),
            pltpu.VMEM((ROWS, 3, 8, 128), BF),
            pltpu.VMEM((COLS, 2, 3, 8, 128), BF),
            pltpu.VMEM((2, 128), F32),
            pltpu.VMEM((COLS, 2, 128), F32),
            pltpu.VMEM((3, 8, 8, 512), F32),
            pltpu.VMEM((512, 384), F32),
            pltpu.VMEM((256, 768), F32),
            pltpu.VMEM((512, 256), BF),
            pltpu.VMEM((256, 128), BF),
            pltpu.SemaphoreType.DMA((7,)),
            pltpu.SemaphoreType.DMA((7,)),
        ],
        compiler_params=pltpu.CompilerParams(collective_id=0, has_side_effects=True),
        name="substep",
    )(adjoint, velocity, control, deriv_x, deriv_y, deriv_z)


def solution(mesh):
    in_specs = (
        P(None, "col", "row", None),
        P(None, "col", "row", None),
        P("row", None),
        P(),
        P(),
        P(),
    )
    out_specs = (P(None, "col", "row", None), P("row", None))
    return jax.shard_map(
        on_device, mesh=mesh, in_specs=in_specs, out_specs=out_specs, check_vma=False
    )
```

```python
import functools

import jax
import jax.numpy as jnp
from jax import lax
from jax.experimental import pallas as pl
from jax.experimental.pallas import tpu as pltpu
from jax.sharding import PartitionSpec as P

BF = jnp.bfloat16
F32 = jnp.float32
ROWS = 32
COLS = 16
MESH = pl.DeviceIdType.MESH


def lanes(chunk):
    return pl.ds(pl.multiple_of(chunk * 128, 128), 128)


def remote(src, dst, send_sem, recv_sem, axis, peer):
    return pltpu.make_async_remote_copy(
        src_ref=src,
        dst_ref=dst,
        send_sem=send_sem,
        recv_sem=recv_sem,
        device_id={axis: peer},
        device_id_type=MESH,
    )


def wait_bytes(ref, sem):
    pltpu.make_async_copy(ref, ref, sem).wait()


def tendency(deriv, visc, speeds, d):
    mixed = speeds[0] * deriv[0] + speeds[1] * deriv[1] + speeds[2] * deriv[2]
    out = []
    for k in range(3):
        value = visc[k] - speeds[d] * deriv[k]
        if k == d:
            value = value - mixed
        out.append(value)
    return out


def kernel(
    adj_in, vel_in, ctl_in, dx_in, dy_in, dz_in, out, cg_out,
    adj, vel, ctl, dx, dy, dz, relay_adj, relay_vel, relay_py, adj_t, vel_t, row_adj, row_vel, col_adj, col_vel,
    py, pz, yback, zback, cg_mine, cg_all,
    base, gy, gz, dyt, dzt, send_sems, recv_sems, load_sems, relay_send, relay_recv,
):
    loads = [
        pltpu.make_async_copy(src, dst, load_sems.at[i])
        for i, (src, dst) in enumerate(
            ((adj_in, adj), (vel_in, vel), (ctl_in, ctl), (dx_in, dx), (dy_in, dy), (dz_in, dz))
        )
    ]
    for load in loads:
        load.start()
    row = lax.axis_index("row")
    col = lax.axis_index("col")
    part, low = row // 8, lax.rem(row, 8)
    ahead, behind = lax.rem(part + 1, 4), lax.rem(part + 3, 4)
    is_relay = lax.rem(row, 2) == 1

    barrier = pltpu.get_barrier_semaphore()

    def greet(axis, me, n):
        def body(i, carry):
            peer = lax.rem(me + i, n)
            pl.semaphore_signal(barrier, inc=1, device_id={axis: peer}, device_id_type=MESH)
            return carry

        lax.fori_loop(1, n, body, 0)

    greet("row", row, ROWS)
    greet("col", col, COLS)

    for load, src, dst in ((loads[0], adj, adj_t), (loads[1], vel, vel_t)):
        load.wait()
        for k in range(3):
            dst[:, k] = jnp.swapaxes(src[k].astype(F32), 0, 1).astype(BF)

    pl.semaphore_wait(barrier, ROWS - 1 + COLS - 1)

    def send_all(which, axis, me, n, view, slots):
        def body(i, carry):
            peer = lax.rem(me + i, n)
            remote(
                view(peer), slots.at[me], send_sems.at[which], recv_sems.at[which], axis, peer
            ).start()
            return carry

        lax.fori_loop(1, n, body, 0)
        pltpu.make_async_copy(view(me), slots.at[me], recv_sems.at[which]).start()

    def send_row(which, view, slots, relayed, stop):
        def send(peer):
            remote(
                view(peer), slots.at[row], send_sems.at[which], recv_sems.at[which], "row", peer
            ).start()

        def opposite(i, carry):
            place = lax.rem(low + i, 8)
            peer = lax.rem(part + 2, 4) * 8 + place

            @pl.when(lax.rem(place, 2) == 0)
            def _():
                send(peer)

            @pl.when(lax.rem(place, 2) == 1)
            def _():
                remote(
                    view(peer), relayed.at[low], send_sems.at[which], relay_recv.at[stop],
                    "row", behind * 8 + place,
                ).start()

            return carry

        def beside(i, carry):
            place = lax.rem(low + i, 8)
            send(ahead * 8 + place)
            send(behind * 8 + place)
            return carry

        def within(i, carry):
            send(part * 8 + lax.rem(low + i, 8))
            return carry

        lax.fori_loop(0, 8, opposite, 0)
        lax.fori_loop(0, 8, beside, 0)
        lax.fori_loop(1, 8, within, 0)
        pltpu.make_async_copy(view(row), slots.at[row], recv_sems.at[which]).start()

    def pass_on(which, slots, relayed, stop):
        @pl.when(is_relay)
        def _():
            wait_bytes(relayed, relay_recv.at[stop])
            remote(
                relayed, slots.at[pl.ds(ahead * 8, 8)], relay_send.at[stop], recv_sems.at[which],
                "row", behind * 8 + low,
            ).start()

    def row_view(ref):
        return lambda r: ref.at[:, r // 4, :, lanes(lax.rem(r, 4))]

    def col_view(ref):
        return lambda c: ref.at[pl.ds(c // 4 * 2, 2), :, :, lanes(lax.rem(c, 4))]

    send_row(0, row_view(adj), row_adj, relay_adj, 0)
    send_row(1, row_view(vel), row_vel, relay_vel, 1)
    send_all(2, "col", col, COLS, col_view(adj_t), col_adj)
    send_all(3, "col", col, COLS, col_view(vel_t), col_vel)

    for load in loads[2:]:
        load.wait()
    for m in range(2):
        dyt[m * 256 : m * 256 + 256, :] = dy[m].astype(F32).T.astype(BF)
        dzt[m * 128 : m * 128 + 128, :] = dz[m].astype(F32).T.astype(BF)

    flat = adj[...].astype(F32).reshape(192, 512).astype(BF)
    for c in range(2):
        cols = slice(c * 256, c * 256 + 256)
        g0 = jnp.dot(flat, dx[0, :, cols], preferred_element_type=F32)
        g1 = jnp.dot(flat, dx[1, :, cols], preferred_element_type=F32)
        speeds = [vel[k, :, :, cols].astype(F32).reshape(64, 256) for k in range(3)]
        parts = tendency(
            [g0[k * 64 : k * 64 + 64] for k in range(3)],
            [g1[k * 64 : k * 64 + 64] for k in range(3)],
            speeds,
            0,
        )
        for k in range(3):
            value = parts[k].astype(BF).astype(F32).reshape(8, 8, 256)
            if k == 0:
                value = value + ctl[:, cols].astype(F32)[None] * adj[0, :, :, cols].astype(F32)
            base[k, :, :, cols] = value

    pass_on(0, row_adj, relay_adj, 0)
    pass_on(1, row_vel, relay_vel, 1)

    wait_bytes(row_adj, recv_sems.at[0])
    lines = jnp.concatenate(
        [row_adj[:, k].astype(F32).reshape(256, 128) for k in range(3)], axis=1
    ).astype(BF)
    gy[...] = jnp.dot(dyt[...], lines, preferred_element_type=F32)
    wait_bytes(row_vel, recv_sems.at[1])
    for c in range(8):
        at = slice(c * 4, c * 4 + 4)
        rows0 = slice(c * 32, c * 32 + 32)
        rows1 = slice(256 + c * 32, 256 + c * 32 + 32)
        parts = tendency(
            [gy[rows0, k * 128 : k * 128 + 128] for k in range(3)],
            [gy[rows1, k * 128 : k * 128 + 128] for k in range(3)],
            [row_vel[at, k].astype(F32).reshape(32, 128) for k in range(3)],
            1,
        )
        for k in range(3):
            py[at, k] = parts[k].reshape(4, 8, 128).astype(BF)
    send_row(4, lambda r: py.at[r], yback, relay_py, 2)

    wait_bytes(col_adj, recv_sems.at[2])
    lines = jnp.concatenate(
        [col_adj[:, y, k].astype(F32).reshape(128, 128) for y in range(2) for k in range(3)],
        axis=1,
    ).astype(BF)
    gz[...] = jnp.dot(dzt[...], lines, preferred_element_type=F32)
    wait_bytes(col_vel, recv_sems.at[3])
    for y in range(2):
        cg_mine[y : y + 1, :] = jnp.sum(
            (col_adj[:, y, 0].astype(F32) * col_vel[:, y, 0].astype(F32)).reshape(128, 128),
            axis=0,
            keepdims=True,
        )
    for c in range(4):
        at = slice(c * 4, c * 4 + 4)
        rows0 = slice(c * 32, c * 32 + 32)
        rows1 = slice(128 + c * 32, 128 + c * 32 + 32)
        for y in range(2):
            first = y * 3
            parts = tendency(
                [gz[rows0, (first + k) * 128 : (first + k + 1) * 128] for k in range(3)],
                [gz[rows1, (first + k) * 128 : (first + k + 1) * 128] for k in range(3)],
                [col_vel[at, y, k].astype(F32).reshape(32, 128) for k in range(3)],
                2,
            )
            for k in range(3):
                pz[at, y, k] = parts[k].reshape(4, 8, 128).astype(BF)
    send_all(5, "col", col, COLS, lambda c: pz.at[c], zback)
    send_all(6, "col", col, COLS, lambda c: cg_mine, cg_all)

    pass_on(4, yback, relay_py, 2)

    wait_bytes(yback, recv_sems.at[4])
    wait_bytes(zback, recv_sems.at[5])
    for x in range(4):
        cols = slice(x * 128, x * 128 + 128)
        for k in range(3):
            span = jnp.stack(
                [zback[(y // 2) * 4 + x, y % 2, k].astype(F32) for y in range(8)], axis=0
            )
            span = jnp.swapaxes(span, 0, 1)
            normal = jnp.stack([yback[z * 4 + x, k].astype(F32) for z in range(8)], axis=0)
            side = (normal + span).astype(BF).astype(F32)
            out[k, :, :, cols] = (base[k, :, :, cols] + side).astype(BF)
    wait_bytes(cg_all, recv_sems.at[6])
    for c in range(COLS):
        yp, x = c // 4, c % 4
        cg_out[yp * 2 : yp * 2 + 2, x * 128 : x * 128 + 128] = cg_all[c]

    for which, slots in enumerate((row_adj, row_vel, col_adj, col_vel, yback, zback, cg_all)):
        wait_bytes(slots.at[pl.ds(0, slots.shape[0] - 1)], send_sems.at[which])

    @pl.when(is_relay)
    def _():
        for stop, relayed in enumerate((relay_adj, relay_vel, relay_py)):
            wait_bytes(relayed, relay_send.at[stop])


def on_device(adjoint, velocity, control, deriv_x, deriv_y, deriv_z):
    vmem = pl.BlockSpec(memory_space=pltpu.VMEM)
    return pl.pallas_call(
        kernel,
        out_shape=(
            jax.ShapeDtypeStruct((3, 8, 8, 512), BF),
            jax.ShapeDtypeStruct((8, 512), F32),
        ),
        in_specs=[pl.BlockSpec(memory_space=pl.ANY)] * 6,
        out_specs=(vmem, vmem),
        scratch_shapes=[
            pltpu.VMEM((3, 8, 8, 512), BF),
            pltpu.VMEM((3, 8, 8, 512), BF),
            pltpu.VMEM((8, 512), BF),
            pltpu.VMEM((2, 512, 512), BF),
            pltpu.VMEM((2, 256, 256), BF),
            pltpu.VMEM((2, 128, 128), BF),
            pltpu.VMEM((8, 3, 8, 128), BF),
            pltpu.VMEM((8, 3, 8, 128), BF),
            pltpu.VMEM((8, 3, 8, 128), BF),
            pltpu.VMEM((8, 3, 8, 512), BF),
            pltpu.VMEM((8, 3, 8, 512), BF),
            pltpu.VMEM((ROWS, 3, 8, 128), BF),
            pltpu.VMEM((ROWS, 3, 8, 128), BF),
            pltpu.VMEM((COLS, 2, 3, 8, 128), BF),
            pltpu.VMEM((COLS, 2, 3, 8, 128), BF),
            pltpu.VMEM((ROWS, 3, 8, 128), BF),
            pltpu.VMEM((COLS, 2, 3, 8, 128), BF),
            pltpu.VMEM((ROWS, 3, 8, 128), BF),
            pltpu.VMEM((COLS, 2, 3, 8, 128), BF),
            pltpu.VMEM((2, 128), F32),
            pltpu.VMEM((COLS, 2, 128), F32),
            pltpu.VMEM((3, 8, 8, 512), F32),
            pltpu.VMEM((512, 384), F32),
            pltpu.VMEM((256, 768), F32),
            pltpu.VMEM((512, 256), BF),
            pltpu.VMEM((256, 128), BF),
            pltpu.SemaphoreType.DMA((7,)),
            pltpu.SemaphoreType.DMA((7,)),
            pltpu.SemaphoreType.DMA((6,)),
            pltpu.SemaphoreType.DMA((3,)),
            pltpu.SemaphoreType.DMA((3,)),
        ],
        compiler_params=pltpu.CompilerParams(collective_id=0, has_side_effects=True),
        name="substep",
    )(adjoint, velocity, control, deriv_x, deriv_y, deriv_z)


def solution(mesh):
    in_specs = (
        P(None, "col", "row", None),
        P(None, "col", "row", None),
        P("row", None),
        P(),
        P(),
        P(),
    )
    out_specs = (P(None, "col", "row", None), P("row", None))
    return jax.shard_map(
        on_device, mesh=mesh, in_specs=in_specs, out_specs=out_specs, check_vma=False
    )
```

```python
import functools

import jax
import jax.numpy as jnp
from jax import lax
from jax.experimental import pallas as pl
from jax.experimental.pallas import tpu as pltpu
from jax.sharding import PartitionSpec as P

BF = jnp.bfloat16
F32 = jnp.float32
MESH = pl.DeviceIdType.MESH


def lanes(chunk):
    return pl.ds(pl.multiple_of(chunk * 128, 128), 128)


def remote(src, dst, send_sem, recv_sem, peer):
    return pltpu.make_async_remote_copy(
        src_ref=src,
        dst_ref=dst,
        send_sem=send_sem,
        recv_sem=recv_sem,
        device_id=peer,
        device_id_type=MESH,
    )


def wait_bytes(ref, sem):
    pltpu.make_async_copy(ref, ref, sem).wait()


def tendency(deriv, visc, speeds, d):
    mixed = speeds[0] * deriv[0] + speeds[1] * deriv[1] + speeds[2] * deriv[2]
    out = []
    for k in range(3):
        value = visc[k] - speeds[d] * deriv[k]
        if k == d:
            value = value - mixed
        out.append(value)
    return out


def kernel(
    adj_in, vel_in, ctl_in, dx_in, dy_in, dz_in, out, cg_out,
    ring_buf, vel, ctl, dx, dy, dz, yin, zin, vy, vz, py, pz, yback, zback,
    cg_part, cg_one, cg_sum, cg_two, cg_mine, cg_all, base, gy, gz, dyt, dzt,
    load_sems, ring_send, ring_recv, send_sems, recv_sems,
):
    row = lax.axis_index("row")
    col = lax.axis_index("col")
    quarter, low = row // 8, lax.rem(row, 8)
    line, step = col // 4, lax.rem(col, 4)
    z = quarter * 4 + step
    adj = ring_buf.at[z]

    loads = [
        pltpu.make_async_copy(src, dst, load_sems.at[i])
        for i, (src, dst) in enumerate(
            ((adj_in, adj), (vel_in, vel), (ctl_in, ctl), (dx_in, dx), (dy_in, dy), (dz_in, dz))
        )
    ]
    for load in loads:
        load.start()

    def at_low(i):
        return (quarter * 8 + lax.rem(low + i, 8), col)

    def at_line(i):
        return (row, lax.rem(line + i, 4) * 4 + step)

    def at_step(i):
        return (row, line * 4 + lax.rem(step + i, 4))

    def at_z(d):
        there = lax.rem(z + d + 16, 16)
        return (there // 4 * 8 + low, line * 4 + lax.rem(there, 4))

    barrier = pltpu.get_barrier_semaphore()
    greeted = [at_z(1), at_z(-1)]
    greeted += [at_low(i) for i in range(1, 8)]
    greeted += [at_line(i) for i in range(1, 4)] + [at_step(i) for i in range(1, 4)]
    for peer in greeted:
        pl.semaphore_signal(barrier, inc=1, device_id=peer, device_id_type=MESH)

    for load in loads:
        load.wait()
    cg_part[...] = jnp.sum(adj[0].astype(F32) * vel[0].astype(F32), axis=0)
    for m in range(2):
        dyt[m * 256 : m * 256 + 256, :] = dy[m].astype(F32).T.astype(BF)
        dzt[m * 128 : m * 128 + 128, :] = dz[m].astype(F32).T
    flat = adj[...].astype(F32).reshape(192, 512).astype(BF)
    for c in range(2):
        cols = slice(c * 256, c * 256 + 256)
        g0 = jnp.dot(flat, dx[0, :, cols], preferred_element_type=F32)
        g1 = jnp.dot(flat, dx[1, :, cols], preferred_element_type=F32)
        parts = tendency(
            [g0[k * 64 : k * 64 + 64] for k in range(3)],
            [g1[k * 64 : k * 64 + 64] for k in range(3)],
            [vel[k, :, :, cols].astype(F32).reshape(64, 256) for k in range(3)],
            0,
        )
        for k in range(3):
            value = parts[k].astype(BF).astype(F32).reshape(8, 8, 256)
            if k == 0:
                value = value + ctl[:, cols].astype(F32)[None] * adj[0, :, :, cols].astype(F32)
            base[k, :, :, cols] = value

    pl.semaphore_wait(barrier, len(greeted))

    def ring(d, s):
        slot = lax.rem(z - d * s + 16, 16)
        if s < 7:
            ref = ring_buf.at[slot]
        else:
            ref = ring_buf.at[slot, :, pl.ds(0 if d > 0 else 4, 4)]
        which = 0 if d > 0 else 1
        return remote(ref, ref, ring_send.at[which], ring_recv.at[which, s], at_z(d))

    def low_sends(which, view, dst, first=0, last=8):
        for i in range(8):
            place = lax.rem(low + i, 8)

            def go(i=i, place=place):
                if i == 0:
                    pltpu.make_async_copy(view(place), dst, recv_sems.at[which]).start()
                else:
                    remote(
                        view(place), dst, send_sems.at[which], recv_sems.at[which], at_low(i)
                    ).start()

            if (first, last) == (0, 8):
                go()
            else:
                pl.when((place >= first) & (place < last))(go)

    def line_sends(which, view, dst):
        for i in range(4):
            place = lax.rem(line + i, 4)
            if i == 0:
                pltpu.make_async_copy(view(place), dst, recv_sems.at[which]).start()
            else:
                remote(
                    view(place), dst, send_sems.at[which], recv_sems.at[which], at_line(i)
                ).start()

    def forward_y(distance, first=0, last=8):
        there = lax.rem(z + distance + 16, 16)
        low_sends(
            0, lambda p: ring_buf.at[there, :, p], yin.at[there // 4 * 8 + low], first, last
        )

    def forward_z(distance):
        there = lax.rem(z + distance + 16, 16)
        line_sends(
            1,
            lambda p: ring_buf.at[there, :, :, :, lanes(p)],
            zin.at[line * 4 + lax.rem(there, 4)],
        )

    ring(1, 0).start()
    ring(-1, 0).start()
    forward_z(0)
    line_sends(3, lambda p: vel.at[:, :, :, lanes(p)], vz.at[line])
    line_sends(6, lambda p: cg_part.at[:, lanes(p)], cg_one.at[line])
    forward_y(0)
    low_sends(2, lambda p: vel.at[:, p], vy.at[low])

    def span_products():
        wait_bytes(zin, recv_sems.at[1])
        wanted = jnp.concatenate(
            [
                dzt[pl.ds(pl.multiple_of(m * 128 + p * 32 + step * 8, 8), 8), :]
                for m in range(2)
                for p in range(4)
            ],
            axis=0,
        ).astype(BF)
        for k in range(3):
            block = jnp.swapaxes(zin[:, k].astype(F32).reshape(128, 8, 128), 0, 1)
            block = jnp.concatenate([block[y] for y in range(8)], axis=1).astype(BF)
            gz[:, k * 1024 : k * 1024 + 1024] = jnp.dot(
                wanted, block, preferred_element_type=F32
            )

    def span_finish(places):
        for p in places:
            def product(m, k):
                at = slice(m * 32 + p * 8, m * 32 + p * 8 + 8)
                tiles = [
                    gz[at, k * 1024 + y * 128 : k * 1024 + y * 128 + 128] for y in range(8)
                ]
                return jnp.swapaxes(jnp.stack(tiles, axis=0), 0, 1)

            parts = tendency(
                [product(0, k) for k in range(3)],
                [product(1, k) for k in range(3)],
                [vz[p, k].astype(F32) for k in range(3)],
                2,
            )
            for k in range(3):
                pz[p, k] = parts[k].astype(BF)

    for s in range(8):
        for d in (1, -1):
            ring(d, s).wait_recv()
            if s < 7:
                ring(d, s + 1).start()
            if s < 3:
                near = step >= s + 1 if d > 0 else step + s + 1 <= 3
                pl.when(near)(functools.partial(forward_z, -d * (s + 1)))
            elif s == 3:
                forward_y(-d * 4)
            elif s == 7:
                forward_y(-d * 8, 0 if d > 0 else 4, 4 if d > 0 else 8)
        if s == 1:
            wait_bytes(cg_one, recv_sems.at[6])
            cg_sum[...] = cg_one[0] + cg_one[1] + cg_one[2] + cg_one[3]
        if s == 2:
            pltpu.make_async_copy(cg_sum, cg_two.at[step], recv_sems.at[7]).start()
            for i in range(1, 4):
                remote(
                    cg_sum, cg_two.at[step], send_sems.at[7], recv_sems.at[7], at_step(i)
                ).start()
        if s == 4:
            span_products()
            wait_bytes(cg_two, recv_sems.at[7])
            cg_mine[...] = cg_two[0] + cg_two[1] + cg_two[2] + cg_two[3]
        if s == 5:
            wait_bytes(vz, recv_sems.at[3])
            span_finish(range(4))
            line_sends(8, lambda p: cg_mine, cg_all.at[line])
        if s == 6:
            line_sends(5, lambda p: pz.at[p], zback.at[line])

    wait_bytes(yin, recv_sems.at[0])
    wait_bytes(vy, recv_sems.at[2])
    wanted = jnp.concatenate(
        [
            dyt[pl.ds(pl.multiple_of(m * 256 + quarter * 64, 64), 64), :]
            for m in range(2)
        ],
        axis=0,
    )
    for k in range(3):
        block = yin[:, k].astype(F32).reshape(256, 512).astype(BF)
        gy[:, k * 512 : k * 512 + 512] = jnp.dot(wanted, block, preferred_element_type=F32)
    for p in range(8):
        for x in range(2):
            cols = slice(x * 256, x * 256 + 256)
            parts = tendency(
                [gy[p * 8 : p * 8 + 8, k * 512 + x * 256 : k * 512 + x * 256 + 256] for k in range(3)],
                [
                    gy[64 + p * 8 : 72 + p * 8, k * 512 + x * 256 : k * 512 + x * 256 + 256]
                    for k in range(3)
                ],
                [vy[p, k, :, cols].astype(F32) for k in range(3)],
                1,
            )
            for k in range(3):
                py[p, k, :, cols] = parts[k].astype(BF)
    low_sends(4, lambda p: py.at[p], yback.at[low])

    wait_bytes(cg_all, recv_sems.at[8])
    for x in range(4):
        cg_out[:, x * 128 : x * 128 + 128] = cg_all[x]
    wait_bytes(zback, recv_sems.at[5])
    wait_bytes(yback, recv_sems.at[4])
    for x in range(4):
        cols = slice(x * 128, x * 128 + 128)
        for k in range(3):
            side = yback[:, k, :, cols].astype(F32) + zback[x, k].astype(F32)
            side = side.astype(BF).astype(F32)
            out[k, :, :, cols] = (base[k, :, :, cols] + side).astype(BF)

    for which in range(2):
        wait_bytes(ring_buf.at[pl.ds(0, 7)], ring_send.at[which])
        wait_bytes(ring_buf.at[0, :, pl.ds(0, 4)], ring_send.at[which])
    sent = (
        yin.at[pl.ds(0, 28)], zin.at[pl.ds(0, 12)], vy.at[pl.ds(0, 7)], vz.at[pl.ds(0, 3)],
        yback.at[pl.ds(0, 7)], zback.at[pl.ds(0, 3)],
        cg_one.at[pl.ds(0, 3)], cg_two.at[pl.ds(0, 3)], cg_all.at[pl.ds(0, 3)],
    )
    for which, ref in enumerate(sent):
        wait_bytes(ref, send_sems.at[which])


def on_device(adjoint, velocity, control, deriv_x, deriv_y, deriv_z):
    vmem = pl.BlockSpec(memory_space=pltpu.VMEM)
    return pl.pallas_call(
        kernel,
        out_shape=(
            jax.ShapeDtypeStruct((3, 8, 8, 512), BF),
            jax.ShapeDtypeStruct((8, 512), F32),
        ),
        in_specs=[pl.BlockSpec(memory_space=pl.ANY)] * 6,
        out_specs=(vmem, vmem),
        scratch_shapes=[
            pltpu.VMEM((16, 3, 8, 8, 512), BF),
            pltpu.VMEM((3, 8, 8, 512), BF),
            pltpu.VMEM((8, 512), BF),
            pltpu.VMEM((2, 512, 512), BF),
            pltpu.VMEM((2, 256, 256), BF),
            pltpu.VMEM((2, 128, 128), BF),
            pltpu.VMEM((32, 3, 8, 512), BF),
            pltpu.VMEM((16, 3, 8, 8, 128), BF),
            pltpu.VMEM((8, 3, 8, 512), BF),
            pltpu.VMEM((4, 3, 8, 8, 128), BF),
            pltpu.VMEM((8, 3, 8, 512), BF),
            pltpu.VMEM((4, 3, 8, 8, 128), BF),
            pltpu.VMEM((8, 3, 8, 512), BF),
            pltpu.VMEM((4, 3, 8, 8, 128), BF),
            pltpu.VMEM((8, 512), F32),
            pltpu.VMEM((4, 8, 128), F32),
            pltpu.VMEM((8, 128), F32),
            pltpu.VMEM((4, 8, 128), F32),
            pltpu.VMEM((8, 128), F32),
            pltpu.VMEM((4, 8, 128), F32),
            pltpu.VMEM((3, 8, 8, 512), F32),
            pltpu.VMEM((128, 1536), F32),
            pltpu.VMEM((64, 3072), F32),
            pltpu.VMEM((512, 256), BF),
            pltpu.VMEM((256, 128), F32),
            pltpu.SemaphoreType.DMA((6,)),
            pltpu.SemaphoreType.DMA((2,)),
            pltpu.SemaphoreType.DMA((2, 8)),
            pltpu.SemaphoreType.DMA((9,)),
            pltpu.SemaphoreType.DMA((9,)),
        ],
        compiler_params=pltpu.CompilerParams(collective_id=0, has_side_effects=True),
        name="substep",
    )(adjoint, velocity, control, deriv_x, deriv_y, deriv_z)


def solution(mesh):
    in_specs = (
        P(None, "col", "row", None),
        P(None, "col", "row", None),
        P("row", None),
        P(),
        P(),
        P(),
    )
    out_specs = (P(None, "col", "row", None), P("row", None))
    return jax.shard_map(
        on_device, mesh=mesh, in_specs=in_specs, out_specs=out_specs, check_vma=False
    )
```

```python
import functools

import jax
import jax.numpy as jnp
from jax import lax
from jax.experimental import pallas as pl
from jax.experimental.pallas import tpu as pltpu
from jax.sharding import PartitionSpec as P

BF = jnp.bfloat16
F32 = jnp.float32
MESH = pl.DeviceIdType.MESH


def lanes(chunk):
    return pl.ds(pl.multiple_of(chunk * 128, 128), 128)


def remote(src, dst, send_sem, recv_sem, peer):
    return pltpu.make_async_remote_copy(
        src_ref=src,
        dst_ref=dst,
        send_sem=send_sem,
        recv_sem=recv_sem,
        device_id=peer,
        device_id_type=MESH,
    )


def wait_bytes(ref, sem):
    pltpu.make_async_copy(ref, ref, sem).wait()


def tendency(deriv, visc, speeds, d):
    mixed = speeds[0] * deriv[0] + speeds[1] * deriv[1] + speeds[2] * deriv[2]
    out = []
    for k in range(3):
        value = visc[k] - speeds[d] * deriv[k]
        if k == d:
            value = value - mixed
        out.append(value)
    return out


def kernel(
    adj_in, vel_in, ctl_in, dx_in, dy_in, dz_in, out, cg_out,
    ring_buf, vel, ctl, dx, dy, dz, yin, zin, vy, vz, py, pz, yback, zback,
    cg_part, cg_one, cg_sum, cg_two, cg_mine, cg_all, base, gy, gz, dyt, dzt,
    load_sems, ring_send, ring_recv, send_sems, recv_sems,
):
    row = lax.axis_index("row")
    col = lax.axis_index("col")
    quarter, low = row // 8, lax.rem(row, 8)
    line, step = col // 4, lax.rem(col, 4)
    z = quarter * 4 + step
    adj = ring_buf.at[z]

    loads = [
        pltpu.make_async_copy(src, dst, load_sems.at[i])
        for i, (src, dst) in enumerate(
            ((adj_in, adj), (vel_in, vel), (ctl_in, ctl), (dx_in, dx), (dy_in, dy), (dz_in, dz))
        )
    ]
    for load in loads:
        load.start()

    def at_low(i):
        return (quarter * 8 + lax.rem(low + i, 8), col)

    def at_line(i):
        return (row, lax.rem(line + i, 4) * 4 + step)

    def at_step(i):
        return (row, line * 4 + lax.rem(step + i, 4))

    def at_z(d):
        there = lax.rem(z + d + 16, 16)
        return (there // 4 * 8 + low, line * 4 + lax.rem(there, 4))

    barrier = pltpu.get_barrier_semaphore()
    greeted = [at_z(1), at_z(-1)]
    greeted += [at_low(i) for i in range(1, 8)]
    greeted += [at_line(i) for i in range(1, 4)] + [at_step(i) for i in range(1, 4)]
    for peer in greeted:
        pl.semaphore_signal(barrier, inc=1, device_id=peer, device_id_type=MESH)

    for load in loads:
        load.wait()
    cg_part[...] = jnp.sum(adj[0].astype(F32) * vel[0].astype(F32), axis=0)
    for m in range(2):
        dyt[m * 256 : m * 256 + 256, :] = dy[m].astype(F32).T.astype(BF)
        dzt[m * 128 : m * 128 + 128, :] = dz[m].astype(F32).T
    flat = adj[...].astype(F32).reshape(192, 512).astype(BF)
    for c in range(2):
        cols = slice(c * 256, c * 256 + 256)
        g0 = jnp.dot(flat, dx[0, :, cols], preferred_element_type=F32)
        g1 = jnp.dot(flat, dx[1, :, cols], preferred_element_type=F32)
        parts = tendency(
            [g0[k * 64 : k * 64 + 64] for k in range(3)],
            [g1[k * 64 : k * 64 + 64] for k in range(3)],
            [vel[k, :, :, cols].astype(F32).reshape(64, 256) for k in range(3)],
            0,
        )
        for k in range(3):
            value = parts[k].astype(BF).astype(F32).reshape(8, 8, 256)
            if k == 0:
                value = value + ctl[:, cols].astype(F32)[None] * adj[0, :, :, cols].astype(F32)
            base[k, :, :, cols] = value

    pl.semaphore_wait(barrier, len(greeted))

    def ring(d, s, k):
        slot = lax.rem(z - d * s + 16, 16)
        if s < 7:
            ref = ring_buf.at[slot, k]
        else:
            ref = ring_buf.at[slot, k, pl.ds(0 if d > 0 else 4, 4)]
        which = 0 if d > 0 else 1
        return remote(ref, ref, ring_send.at[which], ring_recv.at[which, s, k], at_z(d))

    def low_sends(which, view, dst, first=0, last=8):
        for i in range(8):
            place = lax.rem(low + i, 8)

            def go(i=i, place=place):
                if i == 0:
                    pltpu.make_async_copy(view(place), dst, recv_sems.at[which]).start()
                else:
                    remote(
                        view(place), dst, send_sems.at[which], recv_sems.at[which], at_low(i)
                    ).start()

            if (first, last) == (0, 8):
                go()
            else:
                pl.when((place >= first) & (place < last))(go)

    def line_sends(which, view, dst):
        for i in range(4):
            place = lax.rem(line + i, 4)
            if i == 0:
                pltpu.make_async_copy(view(place), dst, recv_sems.at[which]).start()
            else:
                remote(
                    view(place), dst, send_sems.at[which], recv_sems.at[which], at_line(i)
                ).start()

    def forward_y(distance, first=0, last=8):
        there = lax.rem(z + distance + 16, 16)
        low_sends(
            0, lambda p: ring_buf.at[there, :, p], yin.at[there // 4 * 8 + low], first, last
        )

    def forward_z(distance):
        there = lax.rem(z + distance + 16, 16)
        line_sends(
            1,
            lambda p: ring_buf.at[there, :, :, :, lanes(p)],
            zin.at[line * 4 + lax.rem(there, 4)],
        )

    for k in range(3):
        ring(1, 0, k).start()
        ring(-1, 0, k).start()
    forward_z(0)
    line_sends(3, lambda p: vel.at[:, :, :, lanes(p)], vz.at[line])
    line_sends(6, lambda p: cg_part.at[:, lanes(p)], cg_one.at[line])
    forward_y(0)
    low_sends(2, lambda p: vel.at[:, p], vy.at[low])

    def span_products():
        wait_bytes(zin, recv_sems.at[1])
        wanted = jnp.concatenate(
            [
                dzt[pl.ds(pl.multiple_of(m * 128 + p * 32 + step * 8, 8), 8), :]
                for m in range(2)
                for p in range(4)
            ],
            axis=0,
        ).astype(BF)
        for k in range(3):
            block = jnp.swapaxes(zin[:, k].astype(F32).reshape(128, 8, 128), 0, 1)
            block = jnp.concatenate([block[y] for y in range(8)], axis=1).astype(BF)
            gz[:, k * 1024 : k * 1024 + 1024] = jnp.dot(
                wanted, block, preferred_element_type=F32
            )

    def span_finish(places):
        for p in places:
            def product(m, k):
                at = slice(m * 32 + p * 8, m * 32 + p * 8 + 8)
                tiles = [
                    gz[at, k * 1024 + y * 128 : k * 1024 + y * 128 + 128] for y in range(8)
                ]
                return jnp.swapaxes(jnp.stack(tiles, axis=0), 0, 1)

            parts = tendency(
                [product(0, k) for k in range(3)],
                [product(1, k) for k in range(3)],
                [vz[p, k].astype(F32) for k in range(3)],
                2,
            )
            for k in range(3):
                pz[p, k] = parts[k].astype(BF)

    for s in range(8):
        for k in range(3):
            for d in (1, -1):
                ring(d, s, k).wait_recv()
                if s < 7:
                    ring(d, s + 1, k).start()
        for d in (1, -1):
            if s < 3:
                near = step >= s + 1 if d > 0 else step + s + 1 <= 3
                pl.when(near)(functools.partial(forward_z, -d * (s + 1)))
            elif s == 3:
                forward_y(-d * 4)
            elif s == 7:
                forward_y(-d * 8, 0 if d > 0 else 4, 4 if d > 0 else 8)
        if s == 1:
            wait_bytes(cg_one, recv_sems.at[6])
            cg_sum[...] = cg_one[0] + cg_one[1] + cg_one[2] + cg_one[3]
        if s == 2:
            pltpu.make_async_copy(cg_sum, cg_two.at[step], recv_sems.at[7]).start()
            for i in range(1, 4):
                remote(
                    cg_sum, cg_two.at[step], send_sems.at[7], recv_sems.at[7], at_step(i)
                ).start()
        if s == 4:
            span_products()
            wait_bytes(cg_two, recv_sems.at[7])
            cg_mine[...] = cg_two[0] + cg_two[1] + cg_two[2] + cg_two[3]
        if s == 5:
            wait_bytes(vz, recv_sems.at[3])
            span_finish(range(4))
            line_sends(8, lambda p: cg_mine, cg_all.at[line])
        if s == 6:
            line_sends(5, lambda p: pz.at[p], zback.at[line])

    wait_bytes(yin, recv_sems.at[0])
    wait_bytes(vy, recv_sems.at[2])
    wanted = jnp.concatenate(
        [
            dyt[pl.ds(pl.multiple_of(m * 256 + quarter * 64, 64), 64), :]
            for m in range(2)
        ],
        axis=0,
    )
    for k in range(3):
        block = yin[:, k].astype(F32).reshape(256, 512).astype(BF)
        gy[:, k * 512 : k * 512 + 512] = jnp.dot(wanted, block, preferred_element_type=F32)
    for p in range(8):
        for x in range(2):
            cols = slice(x * 256, x * 256 + 256)
            parts = tendency(
                [gy[p * 8 : p * 8 + 8, k * 512 + x * 256 : k * 512 + x * 256 + 256] for k in range(3)],
                [
                    gy[64 + p * 8 : 72 + p * 8, k * 512 + x * 256 : k * 512 + x * 256 + 256]
                    for k in range(3)
                ],
                [vy[p, k, :, cols].astype(F32) for k in range(3)],
                1,
            )
            for k in range(3):
                py[p, k, :, cols] = parts[k].astype(BF)
    low_sends(4, lambda p: py.at[p], yback.at[low])

    wait_bytes(cg_all, recv_sems.at[8])
    for x in range(4):
        cg_out[:, x * 128 : x * 128 + 128] = cg_all[x]
    wait_bytes(zback, recv_sems.at[5])
    wait_bytes(yback, recv_sems.at[4])
    for x in range(4):
        cols = slice(x * 128, x * 128 + 128)
        for k in range(3):
            side = yback[:, k, :, cols].astype(F32) + zback[x, k].astype(F32)
            side = side.astype(BF).astype(F32)
            out[k, :, :, cols] = (base[k, :, :, cols] + side).astype(BF)

    for which in range(2):
        wait_bytes(ring_buf.at[pl.ds(0, 7)], ring_send.at[which])
        wait_bytes(ring_buf.at[0, :, pl.ds(0, 4)], ring_send.at[which])
    sent = (
        yin.at[pl.ds(0, 28)], zin.at[pl.ds(0, 12)], vy.at[pl.ds(0, 7)], vz.at[pl.ds(0, 3)],
        yback.at[pl.ds(0, 7)], zback.at[pl.ds(0, 3)],
        cg_one.at[pl.ds(0, 3)], cg_two.at[pl.ds(0, 3)], cg_all.at[pl.ds(0, 3)],
    )
    for which, ref in enumerate(sent):
        wait_bytes(ref, send_sems.at[which])


def on_device(adjoint, velocity, control, deriv_x, deriv_y, deriv_z):
    vmem = pl.BlockSpec(memory_space=pltpu.VMEM)
    return pl.pallas_call(
        kernel,
        out_shape=(
            jax.ShapeDtypeStruct((3, 8, 8, 512), BF),
            jax.ShapeDtypeStruct((8, 512), F32),
        ),
        in_specs=[pl.BlockSpec(memory_space=pl.ANY)] * 6,
        out_specs=(vmem, vmem),
        scratch_shapes=[
            pltpu.VMEM((16, 3, 8, 8, 512), BF),
            pltpu.VMEM((3, 8, 8, 512), BF),
            pltpu.VMEM((8, 512), BF),
            pltpu.VMEM((2, 512, 512), BF),
            pltpu.VMEM((2, 256, 256), BF),
            pltpu.VMEM((2, 128, 128), BF),
            pltpu.VMEM((32, 3, 8, 512), BF),
            pltpu.VMEM((16, 3, 8, 8, 128), BF),
            pltpu.VMEM((8, 3, 8, 512), BF),
            pltpu.VMEM((4, 3, 8, 8, 128), BF),
            pltpu.VMEM((8, 3, 8, 512), BF),
            pltpu.VMEM((4, 3, 8, 8, 128), BF),
            pltpu.VMEM((8, 3, 8, 512), BF),
            pltpu.VMEM((4, 3, 8, 8, 128), BF),
            pltpu.VMEM((8, 512), F32),
            pltpu.VMEM((4, 8, 128), F32),
            pltpu.VMEM((8, 128), F32),
            pltpu.VMEM((4, 8, 128), F32),
            pltpu.VMEM((8, 128), F32),
            pltpu.VMEM((4, 8, 128), F32),
            pltpu.VMEM((3, 8, 8, 512), F32),
            pltpu.VMEM((128, 1536), F32),
            pltpu.VMEM((64, 3072), F32),
            pltpu.VMEM((512, 256), BF),
            pltpu.VMEM((256, 128), F32),
            pltpu.SemaphoreType.DMA((6,)),
            pltpu.SemaphoreType.DMA((2,)),
            pltpu.SemaphoreType.DMA((2, 8, 3)),
            pltpu.SemaphoreType.DMA((9,)),
            pltpu.SemaphoreType.DMA((9,)),
        ],
        compiler_params=pltpu.CompilerParams(collective_id=0, has_side_effects=True),
        name="substep",
    )(adjoint, velocity, control, deriv_x, deriv_y, deriv_z)


def solution(mesh):
    in_specs = (
        P(None, "col", "row", None),
        P(None, "col", "row", None),
        P("row", None),
        P(),
        P(),
        P(),
    )
    out_specs = (P(None, "col", "row", None), P("row", None))
    return jax.shard_map(
        on_device, mesh=mesh, in_specs=in_specs, out_specs=out_specs, check_vma=False
    )
```

```python
import functools

import jax
import jax.numpy as jnp
from jax import lax
from jax.experimental import pallas as pl
from jax.experimental.pallas import tpu as pltpu
from jax.sharding import PartitionSpec as P

BF = jnp.bfloat16
F32 = jnp.float32
MESH = pl.DeviceIdType.MESH


def lanes(chunk):
    return pl.ds(pl.multiple_of(chunk * 128, 128), 128)


def remote(src, dst, send_sem, recv_sem, peer):
    return pltpu.make_async_remote_copy(
        src_ref=src,
        dst_ref=dst,
        send_sem=send_sem,
        recv_sem=recv_sem,
        device_id=peer,
        device_id_type=MESH,
    )


def wait_bytes(ref, sem):
    pltpu.make_async_copy(ref, ref, sem).wait()


def tendency(deriv, visc, speeds, d):
    mixed = speeds[0] * deriv[0] + speeds[1] * deriv[1] + speeds[2] * deriv[2]
    out = []
    for k in range(3):
        value = visc[k] - speeds[d] * deriv[k]
        if k == d:
            value = value - mixed
        out.append(value)
    return out


def kernel(
    adj_in, vel_in, ctl_in, dx_in, dy_in, dz_in, out, cg_out,
    ring_buf, vel, ctl, dx, dy, dz, yin, zin, vy, vz, py, pz, yback, zback,
    cg_part, cg_one, cg_sum, cg_two, cg_mine, cg_all, base, gy, gz, dyt, dzt,
    load_sems, ring_send, ring_recv, send_sems, recv_sems,
):
    row = lax.axis_index("row")
    col = lax.axis_index("col")
    quarter, low = row // 8, lax.rem(row, 8)
    line, step = col // 4, lax.rem(col, 4)
    z = quarter * 4 + step
    adj = ring_buf.at[z]

    loads = [
        pltpu.make_async_copy(src, dst, load_sems.at[i])
        for i, (src, dst) in enumerate(
            ((adj_in, adj), (vel_in, vel), (ctl_in, ctl), (dx_in, dx), (dy_in, dy), (dz_in, dz))
        )
    ]
    for load in loads:
        load.start()

    def at_low(i):
        return (quarter * 8 + lax.rem(low + i, 8), col)

    def at_line(i):
        return (row, lax.rem(line + i, 4) * 4 + step)

    def at_step(i):
        return (row, line * 4 + lax.rem(step + i, 4))

    def at_z(d):
        there = lax.rem(z + d + 16, 16)
        return (there // 4 * 8 + low, line * 4 + lax.rem(there, 4))

    barrier = pltpu.get_barrier_semaphore()
    greeted = [at_z(1), at_z(-1)]
    greeted += [at_low(i) for i in range(1, 8)]
    greeted += [at_line(i) for i in range(1, 4)] + [at_step(i) for i in range(1, 4)]
    for peer in greeted:
        pl.semaphore_signal(barrier, inc=1, device_id=peer, device_id_type=MESH)

    loads[0].wait()
    def prepare():
        cg_part[...] = jnp.sum(adj[0].astype(F32) * vel[0].astype(F32), axis=0)
        for m in range(2):
            dyt[m * 256 : m * 256 + 256, :] = dy[m].astype(F32).T.astype(BF)
            dzt[m * 128 : m * 128 + 128, :] = dz[m].astype(F32).T

    def stream_part(c):
        flat = adj[...].astype(F32).reshape(192, 512).astype(BF)
        cols = slice(c * 256, c * 256 + 256)
        g0 = jnp.dot(flat, dx[0, :, cols], preferred_element_type=F32)
        g1 = jnp.dot(flat, dx[1, :, cols], preferred_element_type=F32)
        parts = tendency(
            [g0[k * 64 : k * 64 + 64] for k in range(3)],
            [g1[k * 64 : k * 64 + 64] for k in range(3)],
            [vel[k, :, :, cols].astype(F32).reshape(64, 256) for k in range(3)],
            0,
        )
        for k in range(3):
            value = parts[k].astype(BF).astype(F32).reshape(8, 8, 256)
            if k == 0:
                value = value + ctl[:, cols].astype(F32)[None] * adj[0, :, :, cols].astype(F32)
            base[k, :, :, cols] = value

    pl.semaphore_wait(barrier, len(greeted))

    def ring(d, s, piece):
        slot = lax.rem(z - d * s + 16, 16)
        ref = ring_buf.at[slot, piece // 2, pl.ds(piece % 2 * 4, 4)]
        which = 0 if d > 0 else 1
        return remote(ref, ref, ring_send.at[which], ring_recv.at[which, s, piece], at_z(d))

    def carried(d, s):
        return range(6) if s < 4 else range(0 if d > 0 else 1, 6, 2)

    def low_sends(which, view, dst, first=0, last=8):
        for i in range(8):
            place = lax.rem(low + i, 8)

            def go(i=i, place=place):
                if i == 0:
                    pltpu.make_async_copy(view(place), dst, recv_sems.at[which]).start()
                else:
                    remote(
                        view(place), dst, send_sems.at[which], recv_sems.at[which], at_low(i)
                    ).start()

            if (first, last) == (0, 8):
                go()
            else:
                pl.when((place >= first) & (place < last))(go)

    def line_sends(which, view, dst):
        for i in range(4):
            place = lax.rem(line + i, 4)
            if i == 0:
                pltpu.make_async_copy(view(place), dst, recv_sems.at[which]).start()
            else:
                remote(
                    view(place), dst, send_sems.at[which], recv_sems.at[which], at_line(i)
                ).start()

    def forward_y(distance, first=0, last=8, k=None):
        there = lax.rem(z + distance + 16, 16)
        what = slice(None) if k is None else k
        low_sends(
            0,
            lambda p: ring_buf.at[there, what, p],
            yin.at[there // 4 * 8 + low, what],
            first,
            last,
        )

    def forward_z(distance):
        there = lax.rem(z + distance + 16, 16)
        line_sends(
            1,
            lambda p: ring_buf.at[there, :, :, :, lanes(p)],
            zin.at[line * 4 + lax.rem(there, 4)],
        )

    for piece in range(6):
        ring(1, 0, piece).start()
        ring(-1, 0, piece).start()
    for load in loads[1:]:
        load.wait()
    forward_z(0)
    line_sends(3, lambda p: vel.at[:, :, :, lanes(p)], vz.at[line])
    forward_y(0)
    low_sends(2, lambda p: vel.at[:, p], vy.at[low])
    prepare()

    def span_products():
        wait_bytes(zin, recv_sems.at[1])
        wanted = jnp.concatenate(
            [
                dzt[pl.ds(pl.multiple_of(m * 128 + p * 32 + step * 8, 8), 8), :]
                for m in range(2)
                for p in range(4)
            ],
            axis=0,
        ).astype(BF)
        for k in range(3):
            block = jnp.swapaxes(zin[:, k].astype(F32).reshape(128, 8, 128), 0, 1)
            block = jnp.concatenate([block[y] for y in range(8)], axis=1).astype(BF)
            gz[:, k * 1024 : k * 1024 + 1024] = jnp.dot(
                wanted, block, preferred_element_type=F32
            )

    def span_finish(places):
        for p in places:
            def product(m, k):
                at = slice(m * 32 + p * 8, m * 32 + p * 8 + 8)
                tiles = [
                    gz[at, k * 1024 + y * 128 : k * 1024 + y * 128 + 128] for y in range(8)
                ]
                return jnp.swapaxes(jnp.stack(tiles, axis=0), 0, 1)

            parts = tendency(
                [product(0, k) for k in range(3)],
                [product(1, k) for k in range(3)],
                [vz[p, k].astype(F32) for k in range(3)],
                2,
            )
            for k in range(3):
                pz[p, k] = parts[k].astype(BF)

    for s in range(8):
        for piece in range(6):
            for d in (1, -1):
                if piece in carried(d, s):
                    ring(d, s, piece).wait_recv()
                    if s < 7 and piece in carried(d, s + 1):
                        ring(d, s + 1, piece).start()
                    if s == 7:
                        half = piece % 2 * 4
                        forward_y(-d * 8, half, half + 4, piece // 2)
        for d in (1, -1):
            if s < 3:
                near = step >= s + 1 if d > 0 else step + s + 1 <= 3
                pl.when(near)(functools.partial(forward_z, -d * (s + 1)))
            elif s == 3:
                forward_y(-d * 4)
        if s == 0:
            stream_part(0)
            line_sends(6, lambda p: cg_part.at[:, lanes(p)], cg_one.at[line])
        if s == 1:
            stream_part(1)
        if s == 3:
            span_products()
            wait_bytes(vz, recv_sems.at[3])
            wait_bytes(cg_one, recv_sems.at[6])
            cg_sum[...] = cg_one[0] + cg_one[1] + cg_one[2] + cg_one[3]
        if s >= 4:
            span_finish([s - 4])
        if s == 4:
            pltpu.make_async_copy(cg_sum, cg_two.at[step], recv_sems.at[7]).start()
            for i in range(1, 4):
                remote(
                    cg_sum, cg_two.at[step], send_sems.at[7], recv_sems.at[7], at_step(i)
                ).start()
        if s == 6:
            wait_bytes(cg_two, recv_sems.at[7])
            cg_mine[...] = cg_two[0] + cg_two[1] + cg_two[2] + cg_two[3]

    line_sends(5, lambda p: pz.at[p], zback.at[line])
    line_sends(8, lambda p: cg_mine, cg_all.at[line])

    wait_bytes(yin, recv_sems.at[0])
    wait_bytes(vy, recv_sems.at[2])
    wanted = jnp.concatenate(
        [
            dyt[pl.ds(pl.multiple_of(m * 256 + quarter * 64, 64), 64), :]
            for m in range(2)
        ],
        axis=0,
    )
    for k in range(3):
        block = yin[:, k].astype(F32).reshape(256, 512).astype(BF)
        gy[:, k * 512 : k * 512 + 512] = jnp.dot(wanted, block, preferred_element_type=F32)
    for p in range(8):
        for x in range(2):
            cols = slice(x * 256, x * 256 + 256)
            parts = tendency(
                [gy[p * 8 : p * 8 + 8, k * 512 + x * 256 : k * 512 + x * 256 + 256] for k in range(3)],
                [
                    gy[64 + p * 8 : 72 + p * 8, k * 512 + x * 256 : k * 512 + x * 256 + 256]
                    for k in range(3)
                ],
                [vy[p, k, :, cols].astype(F32) for k in range(3)],
                1,
            )
            for k in range(3):
                py[p, k, :, cols] = parts[k].astype(BF)
    low_sends(4, lambda p: py.at[p], yback.at[low])

    wait_bytes(cg_all, recv_sems.at[8])
    for x in range(4):
        cg_out[:, x * 128 : x * 128 + 128] = cg_all[x]
    wait_bytes(zback, recv_sems.at[5])
    wait_bytes(yback, recv_sems.at[4])
    for x in range(4):
        cols = slice(x * 128, x * 128 + 128)
        for k in range(3):
            side = yback[:, k, :, cols].astype(F32) + zback[x, k].astype(F32)
            side = side.astype(BF).astype(F32)
            out[k, :, :, cols] = (base[k, :, :, cols] + side).astype(BF)

    for which in range(2):
        wait_bytes(ring_buf.at[pl.ds(0, 6)], ring_send.at[which])
    sent = (
        yin.at[pl.ds(0, 28)], zin.at[pl.ds(0, 12)], vy.at[pl.ds(0, 7)], vz.at[pl.ds(0, 3)],
        yback.at[pl.ds(0, 7)], zback.at[pl.ds(0, 3)],
        cg_one.at[pl.ds(0, 3)], cg_two.at[pl.ds(0, 3)], cg_all.at[pl.ds(0, 3)],
    )
    for which, ref in enumerate(sent):
        wait_bytes(ref, send_sems.at[which])


def on_device(adjoint, velocity, control, deriv_x, deriv_y, deriv_z):
    vmem = pl.BlockSpec(memory_space=pltpu.VMEM)
    return pl.pallas_call(
        kernel,
        out_shape=(
            jax.ShapeDtypeStruct((3, 8, 8, 512), BF),
            jax.ShapeDtypeStruct((8, 512), F32),
        ),
        in_specs=[pl.BlockSpec(memory_space=pl.ANY)] * 6,
        out_specs=(vmem, vmem),
        scratch_shapes=[
            pltpu.VMEM((16, 3, 8, 8, 512), BF),
            pltpu.VMEM((3, 8, 8, 512), BF),
            pltpu.VMEM((8, 512), BF),
            pltpu.VMEM((2, 512, 512), BF),
            pltpu.VMEM((2, 256, 256), BF),
            pltpu.VMEM((2, 128, 128), BF),
            pltpu.VMEM((32, 3, 8, 512), BF),
            pltpu.VMEM((16, 3, 8, 8, 128), BF),
            pltpu.VMEM((8, 3, 8, 512), BF),
            pltpu.VMEM((4, 3, 8, 8, 128), BF),
            pltpu.VMEM((8, 3, 8, 512), BF),
            pltpu.VMEM((4, 3, 8, 8, 128), BF),
            pltpu.VMEM((8, 3, 8, 512), BF),
            pltpu.VMEM((4, 3, 8, 8, 128), BF),
            pltpu.VMEM((8, 512), F32),
            pltpu.VMEM((4, 8, 128), F32),
            pltpu.VMEM((8, 128), F32),
            pltpu.VMEM((4, 8, 128), F32),
            pltpu.VMEM((8, 128), F32),
            pltpu.VMEM((4, 8, 128), F32),
            pltpu.VMEM((3, 8, 8, 512), F32),
            pltpu.VMEM((128, 1536), F32),
            pltpu.VMEM((64, 3072), F32),
            pltpu.VMEM((512, 256), BF),
            pltpu.VMEM((256, 128), F32),
            pltpu.SemaphoreType.DMA((6,)),
            pltpu.SemaphoreType.DMA((2,)),
            pltpu.SemaphoreType.DMA((2, 8, 6)),
            pltpu.SemaphoreType.DMA((9,)),
            pltpu.SemaphoreType.DMA((9,)),
        ],
        compiler_params=pltpu.CompilerParams(collective_id=0, has_side_effects=True),
        name="substep",
    )(adjoint, velocity, control, deriv_x, deriv_y, deriv_z)


def solution(mesh):
    in_specs = (
        P(None, "col", "row", None),
        P(None, "col", "row", None),
        P("row", None),
        P(),
        P(),
        P(),
    )
    out_specs = (P(None, "col", "row", None), P("row", None))
    return jax.shard_map(
        on_device, mesh=mesh, in_specs=in_specs, out_specs=out_specs, check_vma=False
    )
```

```python
import functools

import jax
import jax.numpy as jnp
from jax import lax
from jax.experimental import pallas as pl
from jax.experimental.pallas import tpu as pltpu
from jax.sharding import PartitionSpec as P

BF = jnp.bfloat16
F32 = jnp.float32
MESH = pl.DeviceIdType.MESH


def lanes(chunk):
    return pl.ds(pl.multiple_of(chunk * 128, 128), 128)


def remote(src, dst, send_sem, recv_sem, peer):
    return pltpu.make_async_remote_copy(
        src_ref=src,
        dst_ref=dst,
        send_sem=send_sem,
        recv_sem=recv_sem,
        device_id=peer,
        device_id_type=MESH,
    )


def wait_bytes(ref, sem):
    pltpu.make_async_copy(ref, ref, sem).wait()


def tendency(deriv, visc, speeds, d):
    mixed = speeds[0] * deriv[0] + speeds[1] * deriv[1] + speeds[2] * deriv[2]
    out = []
    for k in range(3):
        value = visc[k] - speeds[d] * deriv[k]
        if k == d:
            value = value - mixed
        out.append(value)
    return out


def kernel(
    adj_in, vel_in, ctl_in, dx_in, dy_in, dz_in, out, cg_out,
    ring_buf, vel, ctl, dx, dy, dz, yin, zin, vy, vz, py, pz, yback, zback,
    cg_part, cg_one, cg_sum, cg_two, cg_mine, cg_all, base, gy, gz, dyt, dzt,
    load_sems, ring_send, ring_recv, send_sems, recv_sems,
):
    row = lax.axis_index("row")
    col = lax.axis_index("col")
    quarter, low = row // 8, lax.rem(row, 8)
    line, step = col // 4, lax.rem(col, 4)
    z = quarter * 4 + step
    adj = ring_buf.at[z]

    loads = [
        pltpu.make_async_copy(src, dst, load_sems.at[i])
        for i, (src, dst) in enumerate(
            ((adj_in, adj), (vel_in, vel), (ctl_in, ctl), (dx_in, dx), (dy_in, dy), (dz_in, dz))
        )
    ]
    for load in loads:
        load.start()

    def at_low(i):
        return (quarter * 8 + lax.rem(low + i, 8), col)

    def at_line(i):
        return (row, lax.rem(line + i, 4) * 4 + step)

    def at_step(i):
        return (row, line * 4 + lax.rem(step + i, 4))

    def at_z(d):
        there = lax.rem(z + d + 16, 16)
        return (there // 4 * 8 + low, line * 4 + lax.rem(there, 4))

    barrier = pltpu.get_barrier_semaphore()
    greeted = [at_z(1), at_z(-1)]
    greeted += [at_low(i) for i in range(1, 8)]
    greeted += [at_line(i) for i in range(1, 4)] + [at_step(i) for i in range(1, 4)]
    for peer in greeted:
        pl.semaphore_signal(barrier, inc=1, device_id=peer, device_id_type=MESH)

    loads[0].wait()
    def prepare():
        cg_part[...] = jnp.sum(adj[0].astype(F32) * vel[0].astype(F32), axis=0)
        for m in range(2):
            dyt[m * 256 : m * 256 + 256, :] = dy[m].astype(F32).T.astype(BF)
            dzt[m * 128 : m * 128 + 128, :] = dz[m].astype(F32).T

    def stream_part(c):
        flat = adj[...].astype(F32).reshape(192, 512).astype(BF)
        cols = slice(c * 256, c * 256 + 256)
        g0 = jnp.dot(flat, dx[0, :, cols], preferred_element_type=F32)
        g1 = jnp.dot(flat, dx[1, :, cols], preferred_element_type=F32)
        parts = tendency(
            [g0[k * 64 : k * 64 + 64] for k in range(3)],
            [g1[k * 64 : k * 64 + 64] for k in range(3)],
            [vel[k, :, :, cols].astype(F32).reshape(64, 256) for k in range(3)],
            0,
        )
        for k in range(3):
            value = parts[k].astype(BF).astype(F32).reshape(8, 8, 256)
            if k == 0:
                value = value + ctl[:, cols].astype(F32)[None] * adj[0, :, :, cols].astype(F32)
            base[k, :, :, cols] = value

    pl.semaphore_wait(barrier, len(greeted))

    def ring(d, s, piece):
        slot = lax.rem(z - d * s + 16, 16)
        ref = ring_buf.at[slot, piece // 2, pl.ds(piece % 2 * 4, 4)]
        which = 0 if d > 0 else 1
        return remote(ref, ref, ring_send.at[which], ring_recv.at[which, s, piece], at_z(d))

    def carried(d, s):
        return range(6) if s < 4 else range(0 if d > 0 else 1, 6, 2)

    def low_sends(which, view, dst, first=0, last=8):
        for i in range(8):
            place = lax.rem(low + i, 8)

            def go(i=i, place=place):
                if i == 0:
                    pltpu.make_async_copy(view(place), dst, recv_sems.at[which]).start()
                else:
                    remote(
                        view(place), dst, send_sems.at[which], recv_sems.at[which], at_low(i)
                    ).start()

            if (first, last) == (0, 8):
                go()
            else:
                pl.when((place >= first) & (place < last))(go)

    def line_sends(which, view, dst):
        for i in range(4):
            place = lax.rem(line + i, 4)
            if i == 0:
                pltpu.make_async_copy(view(place), dst, recv_sems.at[which]).start()
            else:
                remote(
                    view(place), dst, send_sems.at[which], recv_sems.at[which], at_line(i)
                ).start()

    def forward_y(distance, first=0, last=8, k=None):
        there = lax.rem(z + distance + 16, 16)
        what = slice(None) if k is None else k
        low_sends(
            0,
            lambda p: ring_buf.at[there, what, p],
            yin.at[there // 4 * 8 + low, what],
            first,
            last,
        )

    def forward_z(distance):
        there = lax.rem(z + distance + 16, 16)
        line_sends(
            1,
            lambda p: ring_buf.at[there, :, :, :, lanes(p)],
            zin.at[line * 4 + lax.rem(there, 4)],
        )

    order = {1: (0, 2, 4, 1, 3, 5), -1: (1, 3, 5, 0, 2, 4)}
    for place in range(6):
        for d in (1, -1):
            ring(d, 0, order[d][place]).start()
    for load in loads[1:]:
        load.wait()
    forward_z(0)
    line_sends(3, lambda p: vel.at[:, :, :, lanes(p)], vz.at[line])
    forward_y(0)
    low_sends(2, lambda p: vel.at[:, p], vy.at[low])
    prepare()

    def span_products():
        wait_bytes(zin, recv_sems.at[1])
        wanted = jnp.concatenate(
            [
                dzt[pl.ds(pl.multiple_of(m * 128 + p * 32 + step * 8, 8), 8), :]
                for m in range(2)
                for p in range(4)
            ],
            axis=0,
        ).astype(BF)
        for k in range(3):
            block = jnp.swapaxes(zin[:, k].astype(F32).reshape(128, 8, 128), 0, 1)
            block = jnp.concatenate([block[y] for y in range(8)], axis=1).astype(BF)
            gz[:, k * 1024 : k * 1024 + 1024] = jnp.dot(
                wanted, block, preferred_element_type=F32
            )

    def span_finish(places):
        for p in places:
            def product(m, k):
                at = slice(m * 32 + p * 8, m * 32 + p * 8 + 8)
                tiles = [
                    gz[at, k * 1024 + y * 128 : k * 1024 + y * 128 + 128] for y in range(8)
                ]
                return jnp.swapaxes(jnp.stack(tiles, axis=0), 0, 1)

            parts = tendency(
                [product(0, k) for k in range(3)],
                [product(1, k) for k in range(3)],
                [vz[p, k].astype(F32) for k in range(3)],
                2,
            )
            for k in range(3):
                pz[p, k] = parts[k].astype(BF)

    for s in range(8):
        for place in range(6):
            for d in (1, -1):
                piece = order[d][place]
                if piece in carried(d, s):
                    ring(d, s, piece).wait_recv()
                    if s < 7 and piece in carried(d, s + 1):
                        ring(d, s + 1, piece).start()
                    if s == 7:
                        half = piece % 2 * 4
                        forward_y(-d * 8, half, half + 4, piece // 2)
        for d in (1, -1):
            if s < 3:
                near = step >= s + 1 if d > 0 else step + s + 1 <= 3
                pl.when(near)(functools.partial(forward_z, -d * (s + 1)))
            elif s == 3:
                forward_y(-d * 4)
        if s == 0:
            stream_part(0)
            line_sends(6, lambda p: cg_part.at[:, lanes(p)], cg_one.at[line])
        if s == 1:
            stream_part(1)
        if s == 3:
            span_products()
            wait_bytes(vz, recv_sems.at[3])
            wait_bytes(cg_one, recv_sems.at[6])
            cg_sum[...] = cg_one[0] + cg_one[1] + cg_one[2] + cg_one[3]
        if s >= 4:
            span_finish([s - 4])
        if s == 4:
            pltpu.make_async_copy(cg_sum, cg_two.at[step], recv_sems.at[7]).start()
            for i in range(1, 4):
                remote(
                    cg_sum, cg_two.at[step], send_sems.at[7], recv_sems.at[7], at_step(i)
                ).start()
        if s == 6:
            wait_bytes(cg_two, recv_sems.at[7])
            cg_mine[...] = cg_two[0] + cg_two[1] + cg_two[2] + cg_two[3]

    line_sends(5, lambda p: pz.at[p], zback.at[line])
    line_sends(8, lambda p: cg_mine, cg_all.at[line])

    wait_bytes(yin, recv_sems.at[0])
    wait_bytes(vy, recv_sems.at[2])
    wanted = jnp.concatenate(
        [
            dyt[pl.ds(pl.multiple_of(m * 256 + quarter * 64, 64), 64), :]
            for m in range(2)
        ],
        axis=0,
    )
    for x in range(2):
        cols = slice(x * 256, x * 256 + 256)
        for k in range(3):
            block = yin[:, k, :, cols].astype(F32).reshape(256, 256).astype(BF)
            gy[:, k * 512 + x * 256 : k * 512 + x * 256 + 256] = jnp.dot(
                wanted, block, preferred_element_type=F32
            )
        for p in range(8):
            g = [
                [
                    gy[m * 64 + p * 8 : m * 64 + p * 8 + 8, k * 512 + x * 256 : k * 512 + x * 256 + 256]
                    for k in range(3)
                ]
                for m in range(2)
            ]
            parts = tendency(g[0], g[1], [vy[p, k, :, cols].astype(F32) for k in range(3)], 1)
            for k in range(3):
                py[p, k, :, cols] = parts[k].astype(BF)
        low_sends(4, lambda p: py.at[p, :, :, cols], yback.at[low, :, :, cols])

    wait_bytes(cg_all, recv_sems.at[8])
    for x in range(4):
        cg_out[:, x * 128 : x * 128 + 128] = cg_all[x]
    wait_bytes(zback, recv_sems.at[5])
    wait_bytes(yback, recv_sems.at[4])
    for x in range(4):
        cols = slice(x * 128, x * 128 + 128)
        for k in range(3):
            side = yback[:, k, :, cols].astype(F32) + zback[x, k].astype(F32)
            side = side.astype(BF).astype(F32)
            out[k, :, :, cols] = (base[k, :, :, cols] + side).astype(BF)

    for which in range(2):
        wait_bytes(ring_buf.at[pl.ds(0, 6)], ring_send.at[which])
    sent = (
        yin.at[pl.ds(0, 28)], zin.at[pl.ds(0, 12)], vy.at[pl.ds(0, 7)], vz.at[pl.ds(0, 3)],
        yback.at[pl.ds(0, 7)], zback.at[pl.ds(0, 3)],
        cg_one.at[pl.ds(0, 3)], cg_two.at[pl.ds(0, 3)], cg_all.at[pl.ds(0, 3)],
    )
    for which, ref in enumerate(sent):
        wait_bytes(ref, send_sems.at[which])


def on_device(adjoint, velocity, control, deriv_x, deriv_y, deriv_z):
    vmem = pl.BlockSpec(memory_space=pltpu.VMEM)
    return pl.pallas_call(
        kernel,
        out_shape=(
            jax.ShapeDtypeStruct((3, 8, 8, 512), BF),
            jax.ShapeDtypeStruct((8, 512), F32),
        ),
        in_specs=[pl.BlockSpec(memory_space=pl.ANY)] * 6,
        out_specs=(vmem, vmem),
        scratch_shapes=[
            pltpu.VMEM((16, 3, 8, 8, 512), BF),
            pltpu.VMEM((3, 8, 8, 512), BF),
            pltpu.VMEM((8, 512), BF),
            pltpu.VMEM((2, 512, 512), BF),
            pltpu.VMEM((2, 256, 256), BF),
            pltpu.VMEM((2, 128, 128), BF),
            pltpu.VMEM((32, 3, 8, 512), BF),
            pltpu.VMEM((16, 3, 8, 8, 128), BF),
            pltpu.VMEM((8, 3, 8, 512), BF),
            pltpu.VMEM((4, 3, 8, 8, 128), BF),
            pltpu.VMEM((8, 3, 8, 512), BF),
            pltpu.VMEM((4, 3, 8, 8, 128), BF),
            pltpu.VMEM((8, 3, 8, 512), BF),
            pltpu.VMEM((4, 3, 8, 8, 128), BF),
            pltpu.VMEM((8, 512), F32),
            pltpu.VMEM((4, 8, 128), F32),
            pltpu.VMEM((8, 128), F32),
            pltpu.VMEM((4, 8, 128), F32),
            pltpu.VMEM((8, 128), F32),
            pltpu.VMEM((4, 8, 128), F32),
            pltpu.VMEM((3, 8, 8, 512), F32),
            pltpu.VMEM((128, 1536), F32),
            pltpu.VMEM((64, 3072), F32),
            pltpu.VMEM((512, 256), BF),
            pltpu.VMEM((256, 128), F32),
            pltpu.SemaphoreType.DMA((6,)),
            pltpu.SemaphoreType.DMA((2,)),
            pltpu.SemaphoreType.DMA((2, 8, 6)),
            pltpu.SemaphoreType.DMA((9,)),
            pltpu.SemaphoreType.DMA((9,)),
        ],
        compiler_params=pltpu.CompilerParams(collective_id=0, has_side_effects=True),
        name="substep",
    )(adjoint, velocity, control, deriv_x, deriv_y, deriv_z)


def solution(mesh):
    in_specs = (
        P(None, "col", "row", None),
        P(None, "col", "row", None),
        P("row", None),
        P(),
        P(),
        P(),
    )
    out_specs = (P(None, "col", "row", None), P("row", None))
    return jax.shard_map(
        on_device, mesh=mesh, in_specs=in_specs, out_specs=out_specs, check_vma=False
    )
```
